32 devices in a mesh: dp: 4 (over z), seq: 8 (over y, x, core).
Axes of the slice: x: 2, y: 2, z: 4, core: 2. Of those that a mesh axis runs over, the one named last changes fastest.
Arguments:
- tokens: bfloat16 [2, 4, 512, 1280], P(None, 'dp', 'seq'), may hold values from -6 to 6
- cotangent: bfloat16 [2, 4, 512, 1280], P(None, 'dp', 'seq'), may hold values from -6 to 6
- lengths: int32 [2, 4], P(None, 'dp'), may hold values from 128 to 512, as said below
- gain_attn: bfloat16 [1280], P(('dp', 'seq')), may hold values from 0.5 to 1.5
- w_query: bfloat16 [1280, 1280], P(('dp', 'seq')), may hold values from -0.15625 to 0.15625
- key_weight: bfloat16 [1280, 320], P(('dp', 'seq')), may hold values from -0.15625 to 0.15625
- w_value: bfloat16 [1280, 320], P(('dp', 'seq')), may hold values from -0.15625 to 0.15625
- w_out: bfloat16 [1280, 1280], P(None, ('dp', 'seq')), may hold values from -1.25 to 1.25
- gain_mlp: bfloat16 [1280], P(('dp', 'seq')), may hold values from 0.5 to 1.5
- w_gate: bfloat16 [1280, 3584], P(('dp', 'seq')), may hold values from -0.15625 to 0.15625
- w_up: bfloat16 [1280, 3584], P(('dp', 'seq')), may hold values from -0.15625 to 0.15625
- w_down: bfloat16 [3584, 1280], P(None, ('dp', 'seq')), may hold values from -0.09375 to 0.09375
Outputs:
- layer_out: bfloat16 [2, 4, 512, 1280], P(None, 'dp', 'seq')
- grad_tokens: bfloat16 [2, 4, 512, 1280], P(None, 'dp', 'seq')
- grad_gain_attn: float32 [1280], P(('dp', 'seq'))
- grad_query: float32 [1280, 1280], P(('dp', 'seq'))
- grad_key: float32 [1280, 320], P(('dp', 'seq'))
- grad_value: float32 [1280, 320], P(('dp', 'seq'))
- grad_out: float32 [1280, 1280], P(None, ('dp', 'seq'))
- grad_gain_mlp: float32 [1280], P(('dp', 'seq'))
- grad_gate: float32 [1280, 3584], P(('dp', 'seq'))
- grad_up: float32 [1280, 3584], P(('dp', 'seq'))
- grad_down: float32 [3584, 1280], P(None, ('dp', 'seq'))
The draws below stay inside these ranges and needn't reach their ends.
Inputs may be any that keep to these rules, and one draw needn't show every extreme that they name: `lengths`: each slot holds one sequence of at least a quarter of 512 tokens; in every draw some slot is full and some holds exactly a quarter of 512.
All inputs are finite; a program needn't handle non-finite values.
Results may differ from the reference program's by a relative error of at most 0.017.
Values may be sent and summed in bfloat16 or wider, within the bound.
No kernel may reach another device: no remote copies, remote signals or barrier semaphores. Data moves between devices by JAX's collectives and lax.ppermute only.
A program may use at most 448 MiB of HBM per device.

```python
import math
import jax
import jax.numpy as jnp
from jax import lax

D = 1280
KEY_VALUE_HEADS = 5
QUERY_PER_KEY = 4
HQ = 20
HEAD_SIZE = 64
FF = 3584
QW = 1280
KW = 320
MB = 2
SEQS = 4
SLOT = 512


def draw_lengths(key, part):
    low_end = SLOT // 4
    first_key = jax.random.fold_in(key, 11)
    second_key = jax.random.fold_in(key, 12)
    values = jax.random.randint(first_key, (MB * SEQS,), low_end, SLOT + 1, dtype=jnp.int32)
    order = jax.random.permutation(second_key, MB * SEQS)
    values = values.at[order[0]].set(SLOT)
    values = values.at[order[1]].set(low_end)
    return values.reshape(MB, SEQS)


def levels(key, dims, cuts, least, top_value):
    factor_of = 1.0
    for axis_at, blocks in cuts:
        heights = jax.random.uniform(jax.random.fold_in(jax.random.fold_in(key, 6), axis_at), (blocks,), jnp.float32, least / len(cuts), top_value / len(cuts))
        factor_of = factor_of * jnp.repeat(jnp.exp(heights), dims[axis_at] // blocks).reshape((-1,) + (1,) * (len(dims) - 1 - axis_at))
    return factor_of


def centred(stream_key, shape, scale, reach, shards=(), kind=jnp.bfloat16):
    array = jax.random.normal(stream_key, shape, jnp.float32) * scale
    if len(shards) > 0:
        array = levels(stream_key, shape, shards, -0.22, 0.18) * array
    return jnp.clip(array, min=-reach, max=reach).astype(kind)


def setup_inputs(seed: int = 0) -> dict:
    streams_of = jax.random.split(jax.random.key(seed), 13)
    tokens = centred(streams_of[0], (MB, SEQS, SLOT, D), 1.0, 6.0, ((1, 4), (2, 8)))
    cotangent = centred(streams_of[1], (MB, SEQS, SLOT, D), 1.0, 6.0, ((1, 4), (2, 8)))
    lengths = draw_lengths(jax.random.fold_in(streams_of[12], 71), 0)
    gain_attn = jnp.clip(1.0 + 0.1 * jax.random.normal(streams_of[3], (D,), jnp.float32), 0.5, 1.5).astype(jnp.bfloat16)
    w_query = centred(streams_of[4], (D, QW), D ** -0.5, 0.15625, ((0, 32),))
    key_weight = centred(streams_of[5], (D, KW), D ** -0.5, 0.15625, ((0, 32),))
    w_value = centred(streams_of[6], (D, KW), D ** -0.5, 0.15625, ((0, 32),))
    w_out = centred(streams_of[7], (QW, D), (QW // 64) ** -0.5, 1.25, ((1, 32),))
    gain_mlp = jnp.clip(1.0 + 0.1 * jax.random.normal(streams_of[8], (D,), jnp.float32), 0.5, 1.5).astype(jnp.bfloat16)
    w_gate = centred(streams_of[9], (D, FF), D ** -0.5, 0.15625, ((0, 32),))
    w_up = centred(streams_of[10], (D, FF), D ** -0.5, 0.15625, ((0, 32),))
    w_down = centred(streams_of[11], (FF, D), FF ** -0.5, 0.09375, ((1, 32),))
    return {"tokens": tokens, "cotangent": cotangent, "lengths": lengths, "gain_attn": gain_attn, "w_query": w_query, "key_weight": key_weight, "w_value": w_value, "w_out": w_out, "gain_mlp": gain_mlp, "w_gate": w_gate, "w_up": w_up, "w_down": w_down}


NORM_EPSILON = 1e-05
ROPE_BASE = 10000.0
MASK_FILL = -1e+30

@jax.custom_vjp
def low(v):
    return lax.optimization_barrier(v.astype(jnp.bfloat16)).astype(jnp.float32)

@jax.custom_vjp
def low_back(v):
    return v

def low_keep(v):
    return (low(v), None)

def low_pass(kept, grad):
    return (grad,)

def back_keep(v):
    return (v, None)

def back_low(kept, grad):
    return (low(grad),)
low.defvjp(low_keep, low_pass)
low_back.defvjp(back_keep, back_low)

def product_highest(left, right):
    return jnp.dot(left, right, precision=lax.Precision.HIGHEST)

def rms_norm(rows, gain):
    factor = lax.rsqrt(lax.optimization_barrier(jnp.mean(rows * rows, axis=-1, keepdims=True)) + NORM_EPSILON)
    return rows * factor * gain

def rotary_embed(values, token_positions, heads):
    count = values.shape[0]
    width = values.shape[1] // heads
    half = width // 2
    split = values.reshape(count, heads, width)
    freqs = ROPE_BASE ** (-jnp.arange(half, dtype=jnp.float32) / half)
    angles = token_positions.astype(jnp.float32)[:, None] * freqs[None, :]
    cosine = jnp.cos(angles)[:, None, :]
    sine = jnp.sin(angles)[:, None, :]
    first = split[..., :half]
    second = split[..., half:]
    turned = jnp.concatenate([first * cosine - second * sine, second * cosine + first * sine], axis=-1)
    return turned.reshape(count, heads * width)

def attention_apply(query_heads, key_rows, value_rows, token_positions, slot_length):
    sequence_length = query_heads.shape[0]
    query_block_rows = math.gcd(sequence_length, 512)
    block_list = sequence_length // query_block_rows
    grouped_query = query_heads.reshape(block_list, query_block_rows, KEY_VALUE_HEADS, QUERY_PER_KEY, HEAD_SIZE)
    block_pos = token_positions.reshape(block_list, query_block_rows)
    scale = HEAD_SIZE ** (-0.5)

    def one_block(pieces):
        part, part_pos = pieces
        raw = jnp.einsum('qhgd,khd->hgqk', part, key_rows, precision=lax.Precision.HIGHEST) * scale
        raw = low_back(raw)
        allowed = (token_positions[None, :] <= part_pos[:, None]) & (part_pos[:, None] < slot_length)
        probs = jax.nn.softmax(jnp.where(allowed, raw, MASK_FILL), axis=-1)
        return jnp.einsum('hgqk,khd->qhgd', low(probs), value_rows, precision=lax.Precision.HIGHEST)
    result = lax.map(jax.checkpoint(one_block), (grouped_query, block_pos))
    return result.reshape(sequence_length, HQ * HEAD_SIZE)

def layer(rows, params, token_positions, slot_length):
    gain_attn, w_query, key_weight, w_value, w_out, gain_mlp, w_gate, w_up, w_down = params
    sequence_length = rows.shape[0]
    valid = (token_positions < slot_length).astype(rows.dtype)[:, None]
    normalized_input = low(rms_norm(rows, gain_attn))
    query_heads = low(rotary_embed(low_back(product_highest(normalized_input, w_query)), token_positions, HQ))
    key = low(rotary_embed(low_back(product_highest(normalized_input, key_weight)), token_positions, KEY_VALUE_HEADS))
    value_heads = low_back(low(product_highest(normalized_input, w_value)))
    attention_output = attention_apply(query_heads.reshape(sequence_length, KEY_VALUE_HEADS, QUERY_PER_KEY, HEAD_SIZE), key.reshape(sequence_length, KEY_VALUE_HEADS, HEAD_SIZE), value_heads.reshape(sequence_length, KEY_VALUE_HEADS, HEAD_SIZE), token_positions, slot_length)
    mixed = low_back(low(attention_output * valid))
    residual = rows + low_back(product_highest(mixed, w_out))
    normed_mlp = low(rms_norm(residual, gain_mlp))
    gate = low_back(product_highest(normed_mlp, w_gate))
    up = low_back(product_highest(normed_mlp, w_up))
    activated = low(jax.nn.silu(gate) * up)
    return residual + low_back(product_highest(activated, w_down))

def reference(tokens, cotangent, lengths, gain_attn, w_query, key_weight, w_value, w_out, gain_mlp, w_gate, w_up, w_down):
    params = tuple((weight.astype(jnp.float32) for weight in (gain_attn, w_query, key_weight, w_value, w_out, gain_mlp, w_gate, w_up, w_down)))
    flat_tokens = tokens.astype(jnp.float32).reshape(MB * SEQS, SLOT, D)
    flat_cot = cotangent.astype(jnp.float32).reshape(MB * SEQS, SLOT, D)
    flat_len = lengths.reshape(-1).astype(jnp.int32)
    token_positions = jnp.arange(SLOT, dtype=jnp.int32)

    def step(totals, item):
        rows, grad_rows, slot_length = item
        valid = (token_positions < slot_length).astype(jnp.float32)[:, None]
        output, pull_back = jax.vjp(lambda inputs, weights: layer(inputs, weights, token_positions, slot_length), rows, params)
        grad_inputs, grad_params = pull_back(grad_rows * valid)
        totals = jax.tree.map(lambda total, grad: total + grad, totals, grad_params)
        return (totals, (output.astype(jnp.bfloat16), grad_inputs.astype(jnp.bfloat16)))
    start_totals = jax.tree.map(jnp.zeros_like, params)
    totals, (outputs, grad_inputs) = lax.scan(step, start_totals, (flat_tokens, flat_cot, flat_len))
    layer_out = outputs.reshape(MB, SEQS, SLOT, D)
    grad_tokens = grad_inputs.reshape(MB, SEQS, SLOT, D)
    return (layer_out, grad_tokens, totals[0], totals[1], totals[2], totals[3], totals[4], totals[5], totals[6], totals[7], totals[8])
```

```python
import jax
import jax.numpy as jnp
from jax import lax
from jax.sharding import Mesh
from jax.sharding import PartitionSpec as P

KEY_VALUE_HEADS = 5
QUERY_PER_KEY = 4
HEAD_SIZE = 64
NORM_EPSILON = 1e-05
ROPE_BASE = 10000.0
MASK_FILL = -1e30

TP = 4
CORES = 2
FSDP = ("dp", "ctx", "core")

BF16 = jnp.bfloat16
F32 = jnp.float32


def dot(left, right, left_dim, right_dim):
    return lax.dot_general(
        left, right, (((left_dim,), (right_dim,)), ((), ())), preferred_element_type=F32
    )


def to_peer(value, step):
    return lax.ppermute(value, "tp", [(j, j ^ step) for j in range(TP)])


def swap_core(value):
    return lax.ppermute(value, "core", [(0, 1), (1, 0)])


def gather_tp(block):
    half = block.shape[0] // 2
    first = to_peer(block, 1)
    second = to_peer(block, 2)
    third_top = to_peer(first[:half], 2)
    third_low = to_peer(second[half:], 1)
    return jnp.concatenate([block, first, second, third_top, third_low])


def scatter_tp(partial):
    rows = partial.shape[0] // TP
    low = partial.astype(BF16)
    total = partial[:rows]
    for step in (1, 2, 3):
        total = total + to_peer(low[step * rows : (step + 1) * rows], step).astype(F32)
    return total


def pick(pieces, index):
    low = jnp.where(index % 2 == 0, pieces[0], pieces[1])
    high = jnp.where(index % 2 == 0, pieces[2], pieces[3])
    return jnp.where(index < 2, low, high)


def spread_weights(shard, me):
    blocks = [shard[:, t] for t in range(TP)]
    got = [pick(blocks, me)] + [to_peer(pick(blocks, me ^ k), k) for k in (1, 2, 3)]
    ordered = jnp.stack([pick(got, me ^ t) for t in range(TP)])
    full = lax.all_gather(ordered, FSDP, axis=0, tiled=False)
    rows, cols = shard.shape[0], shard.shape[2]
    groups = full.shape[0] // CORES
    full = full.reshape(groups, CORES, TP, rows, cols)
    return jnp.transpose(full, (0, 2, 1, 3, 4)).reshape(groups * CORES * TP * rows, cols)


def collect_grads(partial, groups, me):
    cols = partial.shape[1]
    rows = partial.shape[0] // (groups * TP * CORES)
    terms = partial.astype(BF16).reshape(groups, TP, CORES, rows, cols)
    terms = jnp.transpose(terms, (0, 2, 1, 3, 4)).reshape(groups * CORES, TP, rows, cols)
    mine = lax.psum_scatter(terms, FSDP, scatter_dimension=0, tiled=False)
    blocks = [mine[t] for t in range(TP)]
    got = [pick(blocks, me)] + [to_peer(pick(blocks, me ^ k), k) for k in (1, 2, 3)]
    return [pick(got, me ^ t).astype(F32) for t in range(TP)]


def rotate(values, cosine, sine, heads):
    count = values.shape[0]
    half = HEAD_SIZE // 2
    split = values.reshape(count, heads, HEAD_SIZE)
    first, second = split[..., :half], split[..., half:]
    return jnp.concatenate(
        [first * cosine - second * sine, second * cosine + first * sine], axis=-1
    )


def norm_stats(rows):
    return lax.rsqrt(jnp.mean(rows * rows, axis=-1, keepdims=True) + NORM_EPSILON)


def norm_back(grad_normed, rows, factor, gain):
    scaled = grad_normed * gain
    mean = jnp.mean(scaled * rows, axis=-1, keepdims=True)
    return factor * scaled - rows * (factor * factor * factor) * mean


def local(groups, tokens, cotangent, lengths, gain_attn, w_query, key_weight, w_value, w_out,
          gain_mlp, w_gate, w_up, w_down):
    core = lax.axis_index("core")
    me = lax.axis_index("tp")
    ctx = lax.axis_index("ctx")
    n_ctx = lax.axis_size("ctx")
    span, width = tokens.shape[2], tokens.shape[3]
    shard_rows = w_gate.shape[0]
    own_rows = span * CORES
    q_cols = w_query.shape[1] // TP
    q_heads = q_cols // HEAD_SIZE
    ff_cols = w_gate.shape[1] // TP

    kv_heads = KEY_VALUE_HEADS
    key_split = key_weight.reshape(shard_rows, kv_heads, HEAD_SIZE)
    value_split = w_value.reshape(shard_rows, kv_heads, HEAD_SIZE)
    kv_pair = lambda split: jnp.stack(
        [split[:, t : t + 2].reshape(shard_rows, 2 * HEAD_SIZE) for t in range(TP)], axis=1
    )
    gains = jnp.stack([gain_attn, gain_mlp], axis=1)
    gains = jnp.pad(gains, ((0, 0), (0, 126)))
    gains = jnp.broadcast_to(gains[:, None], (shard_rows, TP, 128))
    attn_shard = jnp.concatenate(
        [
            w_query.reshape(shard_rows, TP, q_cols),
            kv_pair(key_split),
            kv_pair(value_split),
            jnp.transpose(w_out).reshape(shard_rows, TP, q_cols),
            gains,
        ],
        axis=2,
    )
    ff_shard = jnp.concatenate(
        [
            w_gate.reshape(shard_rows, TP, ff_cols),
            w_up.reshape(shard_rows, TP, ff_cols),
            jnp.transpose(w_down).reshape(shard_rows, TP, ff_cols),
        ],
        axis=2,
    )
    attn_full = spread_weights(attn_shard, me)
    ff_full = spread_weights(ff_shard, me)
    qkv_cols = q_cols + 4 * HEAD_SIZE
    w_qkv = attn_full[:, :qkv_cols]
    w_out_t = attn_full[:, qkv_cols : qkv_cols + q_cols]
    gain_rows = jnp.transpose(attn_full[:, qkv_cols + q_cols :])[:8].astype(F32)
    full_gain_attn, full_gain_mlp = gain_rows[0:1], gain_rows[1:2]
    w_gate_up = ff_full[:, : 2 * ff_cols]
    w_down_t = ff_full[:, 2 * ff_cols :]

    first_core = core == 0
    pair = jnp.stack([tokens[:, 0], cotangent[:, 0]], axis=1)
    keep = jnp.where(first_core, pair[0], pair[1])
    got = swap_core(jnp.where(first_core, pair[1], pair[0]))
    own = jnp.concatenate(
        [jnp.where(first_core, keep, got), jnp.where(first_core, got, keep)], axis=1
    )
    slot_length = jnp.where(first_core, lengths[0, 0], lengths[1, 0])
    chip_rows = jnp.arange(own_rows, dtype=jnp.int32)
    own_pos = (ctx * TP + me) * own_rows + chip_rows
    positions = jnp.concatenate([(ctx * TP + (me ^ k)) * own_rows + chip_rows for k in range(TP)])
    own_valid = own_pos[:, None] < slot_length
    valid = positions[:, None] < slot_length
    rows_low = own[0]
    grad_y_low = jnp.where(own_valid, own[1], jnp.zeros_like(own[1]))
    rows = rows_low.astype(F32)
    grad_y = grad_y_low.astype(F32)
    all_rows = gather_tp(rows_low).astype(F32)
    all_grad_y = gather_tp(grad_y_low)

    factor_attn = norm_stats(all_rows)
    normed_low = (all_rows * factor_attn * full_gain_attn).astype(BF16)
    qkv = dot(normed_low, w_qkv, 1, 0)
    half = HEAD_SIZE // 2
    freqs = ROPE_BASE ** (-jnp.arange(half, dtype=F32) / half)
    angles = positions.astype(F32)[:, None] * freqs[None, :]
    cosine, sine = jnp.cos(angles)[:, None, :], jnp.sin(angles)[:, None, :]
    turned = rotate(qkv[:, : q_cols + 2 * HEAD_SIZE], cosine, sine, q_heads + 2).astype(BF16)
    query = jnp.transpose(turned[:, :q_heads], (1, 0, 2))
    pairs = jnp.concatenate(
        [turned[:, q_heads:], qkv[:, q_cols + 2 * HEAD_SIZE :].astype(BF16).reshape(-1, 2, HEAD_SIZE)],
        axis=1,
    )
    pairs = jnp.transpose(pairs, (1, 0, 2))
    key_pos = positions
    if n_ctx > 1:
        pairs = lax.all_gather(pairs, "ctx", axis=1, tiled=True)
        key_pos = lax.all_gather(positions.astype(F32), "ctx", axis=0, tiled=True).astype(jnp.int32)
    second_slot = [None] + [i >= TP - me for i in range(1, q_heads - 1)] + [None]

    def expand(two):
        middle = [jnp.where(second_slot[i], two[1], two[0]) for i in range(1, q_heads - 1)]
        return jnp.stack([two[0], *middle, two[1]])

    def contract(many):
        zero = jnp.zeros_like(many[0])
        low, high = many[0], many[q_heads - 1]
        for i in range(1, q_heads - 1):
            low = low + jnp.where(second_slot[i], zero, many[i])
            high = high + jnp.where(second_slot[i], many[i], zero)
        return jnp.stack([low, high])

    keys, values = expand(pairs[:2]), expand(pairs[2:])
    scale = HEAD_SIZE ** (-0.5)
    scores = jnp.einsum("hqd,hkd->hqk", query, keys, preferred_element_type=F32) * scale
    scores = jnp.where(key_pos[None, None, :] <= positions[None, :, None], scores, MASK_FILL)
    probs = jax.nn.softmax(scores, axis=-1)
    probs_low = probs.astype(BF16)
    mixed = jnp.einsum("hqk,hkd->qhd", probs_low, values, preferred_element_type=F32)
    mixed = jnp.where(valid, mixed.reshape(-1, q_cols), 0.0).astype(BF16)
    residual = rows + scatter_tp(dot(mixed, w_out_t, 1, 1))

    factor_mlp = norm_stats(residual)
    normed_mlp_low = gather_tp((residual * factor_mlp * full_gain_mlp).astype(BF16))
    gate_up = dot(normed_mlp_low, w_gate_up, 1, 0)
    gate, up = gate_up[:, :ff_cols], gate_up[:, ff_cols:]
    sig = jax.nn.sigmoid(gate)
    activated_low = (gate * sig * up).astype(BF16)
    output = residual + scatter_tp(dot(activated_low, w_down_t, 1, 1))

    grad_act = dot(all_grad_y, w_down_t, 1, 0)
    grad_gate = grad_act * up * sig * (1.0 + gate * (1.0 - sig))
    grad_up = grad_act * gate * sig
    grad_gu_low = jnp.concatenate([grad_gate.astype(BF16), grad_up.astype(BF16)], axis=1)
    grad_normed_mlp = scatter_tp(dot(grad_gu_low, w_gate_up, 1, 1))
    ff_terms = jnp.concatenate(
        [dot(normed_mlp_low, grad_gu_low, 0, 0).astype(BF16), dot(all_grad_y, activated_low, 0, 0).astype(BF16)],
        axis=1,
    )
    ff_grads = collect_grads(ff_terms, groups, me)
    gain_mlp_terms = jnp.sum(grad_normed_mlp * residual * factor_mlp, axis=0)
    grad_res = grad_y + norm_back(grad_normed_mlp, residual, factor_mlp, full_gain_mlp)

    grad_res_low = gather_tp(grad_res.astype(BF16))
    grad_mixed = dot(grad_res_low, w_out_t, 1, 0)
    grad_attended = jnp.where(valid, grad_mixed, 0.0).astype(BF16).reshape(-1, q_heads, HEAD_SIZE)
    grad_attended = jnp.transpose(grad_attended, (1, 0, 2))
    grad_probs = jnp.einsum("hqd,hkd->hqk", grad_attended, values, preferred_element_type=F32)
    inner = jnp.sum(probs * grad_probs, axis=-1, keepdims=True)
    grad_scores = (probs * (grad_probs - inner)).astype(BF16)
    grad_query = jnp.einsum("hqk,hkd->qhd", grad_scores, keys, preferred_element_type=F32) * scale
    grad_keys = contract(
        jnp.einsum("hqk,hqd->hkd", grad_scores, query, preferred_element_type=F32) * scale
    )
    grad_values = contract(
        jnp.einsum("hqk,hqd->hkd", probs_low, grad_attended, preferred_element_type=F32)
    )
    grad_pairs = jnp.concatenate([grad_keys, grad_values])
    if n_ctx > 1:
        grad_pairs = lax.psum_scatter(grad_pairs, "ctx", scatter_dimension=1, tiled=True)
    grad_pairs = jnp.transpose(grad_pairs, (1, 0, 2))
    grad_turned = jnp.concatenate([grad_query, grad_pairs[:, :2]], axis=1)
    grad_lin = rotate(grad_turned, cosine, -sine, q_heads + 2)
    grad_qkv_low = (
        jnp.concatenate([grad_lin, grad_pairs[:, 2:]], axis=1).astype(BF16).reshape(-1, qkv_cols)
    )
    grad_normed_part = dot(grad_qkv_low, w_qkv, 1, 1)
    gain_attn_terms = jnp.sum(grad_normed_part * all_rows * factor_attn, axis=0)
    grad_normed = scatter_tp(grad_normed_part)
    grad_rows = grad_res + norm_back(grad_normed, rows, factor_attn[:own_rows], full_gain_attn)

    gain_cols = jnp.transpose(
        jnp.pad(jnp.stack([gain_attn_terms, gain_mlp_terms]), ((0, 126), (0, 0))).astype(BF16)
    )
    attn_terms = jnp.concatenate(
        [
            dot(normed_low, grad_qkv_low, 0, 0).astype(BF16),
            dot(grad_res_low, mixed, 0, 0).astype(BF16),
            gain_cols,
        ],
        axis=1,
    )
    attn_grads = collect_grads(attn_terms, groups, me)

    def give_back(own_out):
        top, low = own_out[:span], own_out[span:]
        keep = jnp.where(first_core, top, low)
        got = swap_core(jnp.where(first_core, low, top))
        return jnp.stack([jnp.where(first_core, keep, got), jnp.where(first_core, got, keep)])[:, None]

    layer_out = give_back(output.astype(BF16))
    grad_tokens = give_back(grad_rows.astype(BF16))
    grad_query_w = jnp.concatenate([g[:, :q_cols] for g in attn_grads], axis=1)

    def kv_grad(start):
        parts = [g[:, start : start + 2 * HEAD_SIZE].reshape(shard_rows, 2, HEAD_SIZE) for g in attn_grads]
        heads = [parts[0][:, 0]]
        heads += [parts[t - 1][:, 1] + parts[t][:, 0] for t in range(1, TP)]
        heads += [parts[TP - 1][:, 1]]
        return jnp.concatenate(heads, axis=1)

    grad_key_w = kv_grad(q_cols)
    grad_value_w = kv_grad(q_cols + 2 * HEAD_SIZE)
    grad_out_w = jnp.transpose(
        jnp.concatenate([g[:, qkv_cols : qkv_cols + q_cols] for g in attn_grads], axis=1)
    )
    gain_sums = sum(g[:, qkv_cols + q_cols : qkv_cols + q_cols + 2] for g in attn_grads)
    grad_gate_w = jnp.concatenate([g[:, :ff_cols] for g in ff_grads], axis=1)
    grad_up_w = jnp.concatenate([g[:, ff_cols : 2 * ff_cols] for g in ff_grads], axis=1)
    grad_down_w = jnp.transpose(jnp.concatenate([g[:, 2 * ff_cols :] for g in ff_grads], axis=1))
    return (
        layer_out,
        grad_tokens,
        gain_sums[:, 0],
        grad_query_w,
        grad_key_w,
        grad_value_w,
        grad_out_w,
        gain_sums[:, 1],
        grad_gate_w,
        grad_up_w,
        grad_down_w,
    )


def solution(mesh):
    n_dp, n_seq = mesh.shape["dp"], mesh.shape["seq"]
    n_ctx = n_seq // (TP * CORES)
    fine = Mesh(mesh.devices.reshape(n_dp, n_ctx, TP, CORES), ("dp", "ctx", "tp", "core"))
    seq = ("ctx", "tp", "core")
    model = ("dp", *seq)
    rows = P(None, "dp", seq, None)

    def body(*arrays):
        return local(n_dp * n_ctx, *arrays)

    return jax.shard_map(
        body,
        mesh=fine,
        in_specs=(
            rows, rows, P(None, "dp"), P(model), P(model, None), P(model, None), P(model, None),
            P(None, model), P(model), P(model, None), P(model, None), P(None, model),
        ),
        out_specs=(
            rows, rows, P(model), P(model, None), P(model, None), P(model, None), P(None, model),
            P(model), P(model, None), P(model, None), P(None, model),
        ),
        check_vma=False,
    )
```

```python
import jax
import jax.numpy as jnp
from jax import lax
from jax.experimental import pallas as pl
from jax.experimental.pallas import tpu as pltpu
from jax.sharding import Mesh
from jax.sharding import PartitionSpec as P

KEY_VALUE_HEADS = 5
QUERY_PER_KEY = 4
HEAD_SIZE = 64
NORM_EPSILON = 1e-05
ROPE_BASE = 10000.0
MASK_FILL = -1e30

TP = 4
CORES = 2
FSDP = ("dp", "ctx", "core")

FF_STEP = 256


BF16 = jnp.bfloat16
F32 = jnp.float32


def dot(left, right, left_dim, right_dim):
    return lax.dot_general(
        left, right, (((left_dim,), (right_dim,)), ((), ())), preferred_element_type=F32
    )


def to_peer(value, step):
    return lax.ppermute(value, "tp", [(j, j ^ step) for j in range(TP)])


def swap_core(value):
    return lax.ppermute(value, "core", [(0, 1), (1, 0)])


def gather_tp(block):
    return jnp.concatenate([block] + [to_peer(block, k) for k in (1, 2, 3)])


def scatter_tp(partial):
    rows = partial.shape[0] // TP
    low = partial.astype(BF16)
    total = partial[:rows].astype(F32)
    for step in (1, 2, 3):
        total = total + to_peer(low[step * rows : (step + 1) * rows], step).astype(F32)
    return total


def pick(pieces, index):
    low = jnp.where(index % 2 == 0, pieces[0], pieces[1])
    high = jnp.where(index % 2 == 0, pieces[2], pieces[3])
    return jnp.where(index < 2, low, high)


def exchange_tp(blocks, me):
    got = [pick(blocks, me)] + [to_peer(pick(blocks, me ^ k), k) for k in (1, 2, 3)]
    return [pick(got, me ^ t) for t in range(TP)]


def ff_kernel(h_ref, y_ref, w_hbm, down_ref, dh_ref, dw_hbm, w_ref, dw_ref, down_acc, dh_acc, in_sem, out_sem):
    hidden = w_ref.shape[1] // 3
    starts = list(range(0, hidden, FF_STEP))

    def fetch(i, k):
        at = pl.ds(k * hidden + starts[i], min(FF_STEP, hidden - starts[i]))
        return pltpu.make_async_copy(w_hbm.at[:, at], w_ref.at[:, at], in_sem.at[i, k])

    def flush(i, k):
        at = pl.ds(k * hidden + starts[i], min(FF_STEP, hidden - starts[i]))
        return pltpu.make_async_copy(dw_ref.at[:, at], dw_hbm.at[:, at], out_sem.at[i, k])

    for i in range(len(starts)):
        for k in range(3):
            fetch(i, k).start()
    rows, rows_t = h_ref[...], h_ref[...].T
    grad, grad_t = y_ref[...], y_ref[...].T
    for i, start in enumerate(starts):
        size = min(FF_STEP, hidden - start)
        for k in range(3):
            fetch(i, k).wait()
        cols = [pl.ds(k * hidden + start, size) for k in range(3)]
        w_gu = jnp.concatenate([w_ref[:, cols[0]], w_ref[:, cols[1]]], axis=1)
        w_down = w_ref[:, cols[2]]
        gate_up = dot(rows, w_gu, 1, 0)
        grad_act = dot(grad, w_down, 1, 0)
        gate, up = gate_up[:, :size], gate_up[:, size:]
        sig = jax.nn.sigmoid(gate)
        act = gate * sig
        activated = (act * up).astype(BF16)
        grad_gate = (grad_act * up * (sig + act * (1.0 - sig))).astype(BF16)
        grad_up = (grad_act * act).astype(BF16)
        grad_gu = jnp.concatenate([grad_gate, grad_up], axis=1)
        terms = dot(rows_t, grad_gu, 1, 0).astype(BF16)
        dw_ref[:, cols[0]] = terms[:, :size]
        dw_ref[:, cols[1]] = terms[:, size:]
        dw_ref[:, cols[2]] = dot(grad_t, activated, 1, 0).astype(BF16)
        for k in range(3):
            flush(i, k).start()
        down = dot(activated, w_down, 1, 1)
        back = dot(grad_gu, w_gu, 1, 1)
        last = i == len(starts) - 1
        down = down if i == 0 else down_acc[...] + down
        back = back if i == 0 else dh_acc[...] + back
        if last:
            down_ref[...] = down.astype(BF16)
            dh_ref[...] = back.astype(BF16)
        else:
            down_acc[...] = down
            dh_acc[...] = back
    for i in range(len(starts)):
        for k in range(3):
            flush(i, k).wait()


def feed_forward(rows_low, grad_low, weights):
    count, width = rows_low.shape
    steps = -(-(weights.shape[1] // 3) // FF_STEP)
    vmem, hbm = pl.BlockSpec(memory_space=pltpu.VMEM), pl.BlockSpec(memory_space=pl.ANY)
    return pl.pallas_call(
        ff_kernel,
        in_specs=[vmem, vmem, hbm],
        out_specs=[vmem, vmem, hbm],
        out_shape=[
            jax.ShapeDtypeStruct((count, width), BF16),
            jax.ShapeDtypeStruct((count, width), BF16),
            jax.ShapeDtypeStruct(weights.shape, BF16),
        ],
        scratch_shapes=[
            pltpu.VMEM(weights.shape, BF16),
            pltpu.VMEM(weights.shape, BF16),
            pltpu.VMEM((count, width), F32),
            pltpu.VMEM((count, width), F32),
            pltpu.SemaphoreType.DMA((steps, 3)),
            pltpu.SemaphoreType.DMA((steps, 3)),
        ],
        compiler_params=pltpu.CompilerParams(vmem_limit_bytes=48 << 20),
        cost_estimate=pl.CostEstimate(
            flops=6 * count * width * weights.shape[1],
            bytes_accessed=4 * width * weights.shape[1] + 8 * count * width,
            transcendentals=count * weights.shape[1] // 3,
        ),
        name="feed_forward",
    )(rows_low, grad_low, weights)


def width_order(rows_low, groups):
    width = rows_low.shape[1]
    rows = width // (groups * TP * CORES)
    at = jnp.arange(width, dtype=jnp.int32)
    row, rest = at % rows, at // rows
    chip, rest = rest % TP, rest // TP
    core, group = rest % CORES, rest // CORES
    model = ((group * TP + chip) * CORES + core) * rows + row
    return (at[:, None] == model[None, :]).astype(BF16)


def rotate(values, cosine, sine, heads):
    count = values.shape[0]
    half = HEAD_SIZE // 2
    split = values.reshape(count, heads, HEAD_SIZE)
    first, second = split[..., :half], split[..., half:]
    return jnp.concatenate(
        [first * cosine - second * sine, second * cosine + first * sine], axis=-1
    )


def norm_stats(rows):
    return lax.rsqrt(jnp.mean(rows * rows, axis=-1, keepdims=True) + NORM_EPSILON)


def norm_back(grad_normed, rows, factor):
    mean = jnp.mean(grad_normed * rows, axis=-1, keepdims=True)
    return factor * grad_normed - rows * (factor * factor * factor) * mean


def local(groups, tokens, cotangent, lengths, gain_attn, w_query, key_weight, w_value, w_out,
          gain_mlp, w_gate, w_up, w_down):
    core = lax.axis_index("core")
    me = lax.axis_index("tp")
    ctx = lax.axis_index("ctx")
    n_ctx = lax.axis_size("ctx")
    span, width = tokens.shape[2], tokens.shape[3]
    shard_rows = w_gate.shape[0]
    own_rows = span * CORES
    q_cols = w_query.shape[1] // TP
    q_heads = q_cols // HEAD_SIZE
    ff_cols = w_gate.shape[1] // TP

    pair_cols = 2 * HEAD_SIZE
    qkv_cols = q_cols + 2 * pair_cols
    gain_attn_col = gain_attn.astype(F32)[:, None]
    gain_mlp_col = gain_mlp.astype(F32)[:, None]
    out_shard, down_shard = jnp.transpose(w_out), jnp.transpose(w_down)

    def part(array, t, step, size):
        return array[:, t * step : t * step + size]

    def scaled(array, gain):
        return (array.astype(F32) * gain).astype(BF16)

    attn_blocks = [
        jnp.concatenate(
            [
                scaled(part(w_query, t, q_cols, q_cols), gain_attn_col),
                scaled(part(key_weight, t, HEAD_SIZE, pair_cols), gain_attn_col),
                scaled(part(w_value, t, HEAD_SIZE, pair_cols), gain_attn_col),
                part(out_shard, t, q_cols, q_cols),
            ],
            axis=1,
        )
        for t in range(TP)
    ]
    ff_blocks = [
        jnp.concatenate(
            [
                scaled(part(w_gate, t, ff_cols, ff_cols), gain_mlp_col),
                scaled(part(w_up, t, ff_cols, ff_cols), gain_mlp_col),
                part(down_shard, t, ff_cols, ff_cols),
            ],
            axis=1,
        )
        for t in range(TP)
    ]
    attn_rows = jnp.concatenate(exchange_tp(attn_blocks, me))
    attn_rows, *ff_blocks = lax.optimization_barrier((attn_rows, *ff_blocks))
    ff_rows = jnp.concatenate(exchange_tp(ff_blocks, me))
    attn_full = lax.all_gather(attn_rows, FSDP, axis=0, tiled=True)
    ff_full = lax.all_gather(ff_rows, FSDP, axis=0, tiled=True)
    w_qkv, w_out_t = attn_full[:, :qkv_cols], attn_full[:, qkv_cols:]

    first_core = core == 0
    pair = jnp.stack([tokens[:, 0], cotangent[:, 0]], axis=1)
    keep = jnp.where(first_core, pair[0], pair[1])
    got = swap_core(jnp.where(first_core, pair[1], pair[0]))
    own = jnp.concatenate(
        [jnp.where(first_core, keep, got), jnp.where(first_core, got, keep)], axis=1
    )
    slot_length = jnp.where(first_core, lengths[0, 0], lengths[1, 0])
    chip_rows = jnp.arange(own_rows, dtype=jnp.int32)
    own_pos = (ctx * TP + me) * own_rows + chip_rows
    positions = jnp.concatenate([(ctx * TP + (me ^ k)) * own_rows + chip_rows for k in range(TP)])
    own_valid = own_pos[:, None] < slot_length
    valid = positions[:, None] < slot_length
    order = width_order(own[0], groups)
    rows_low = dot(own[0], order, 1, 0).astype(BF16)
    grad_y_low = jnp.where(own_valid, dot(own[1], order, 1, 0), 0.0).astype(BF16)
    rows = rows_low.astype(F32)
    grad_y = grad_y_low.astype(F32)
    all_rows = gather_tp(rows_low)
    grad_y_low, all_rows = lax.optimization_barrier((grad_y_low, all_rows))
    all_rows = all_rows.astype(F32)
    all_grad_y = gather_tp(grad_y_low)

    factor_attn = norm_stats(all_rows)
    normed_low = (all_rows * factor_attn).astype(BF16)
    qkv = dot(normed_low, w_qkv, 1, 0)
    half = HEAD_SIZE // 2
    freqs = ROPE_BASE ** (-jnp.arange(half, dtype=F32) / half)
    angles = positions.astype(F32)[:, None] * freqs[None, :]
    cosine, sine = jnp.cos(angles)[:, None, :], jnp.sin(angles)[:, None, :]
    turned = rotate(qkv[:, : q_cols + 2 * HEAD_SIZE], cosine, sine, q_heads + 2).astype(BF16)
    query = jnp.transpose(turned[:, :q_heads], (1, 0, 2))
    pairs = jnp.concatenate(
        [turned[:, q_heads:], qkv[:, q_cols + 2 * HEAD_SIZE :].astype(BF16).reshape(-1, 2, HEAD_SIZE)],
        axis=1,
    )
    pairs = jnp.transpose(pairs, (1, 0, 2))
    key_pos = positions
    if n_ctx > 1:
        pairs = lax.all_gather(pairs, "ctx", axis=1, tiled=True)
        key_pos = lax.all_gather(positions.astype(F32), "ctx", axis=0, tiled=True).astype(jnp.int32)
    second_slot = [None] + [i >= TP - me for i in range(1, q_heads - 1)] + [None]

    def expand(two):
        middle = [jnp.where(second_slot[i], two[1], two[0]) for i in range(1, q_heads - 1)]
        return jnp.stack([two[0], *middle, two[1]])

    def contract(many):
        zero = jnp.zeros_like(many[0])
        low, high = many[0], many[q_heads - 1]
        for i in range(1, q_heads - 1):
            low = low + jnp.where(second_slot[i], zero, many[i])
            high = high + jnp.where(second_slot[i], many[i], zero)
        return jnp.stack([low, high])

    keys, values = expand(pairs[:2]), expand(pairs[2:])
    scale = HEAD_SIZE ** (-0.5)
    scores = jnp.einsum("hqd,hkd->hqk", query, keys, preferred_element_type=F32) * scale
    scores = jnp.where(key_pos[None, None, :] <= positions[None, :, None], scores, MASK_FILL)
    probs = jax.nn.softmax(scores, axis=-1)
    probs_low = probs.astype(BF16)
    mixed = jnp.einsum("hqk,hkd->qhd", probs_low, values, preferred_element_type=F32)
    mixed = jnp.where(valid, mixed.reshape(-1, q_cols), 0.0).astype(BF16)
    out_part = dot(mixed, w_out_t, 1, 1).astype(BF16)
    out_part, all_grad_y = lax.optimization_barrier((out_part, all_grad_y))
    residual = rows + scatter_tp(out_part)

    factor_mlp = norm_stats(residual)
    normed_mlp_low = gather_tp((residual * factor_mlp).astype(BF16))
    down_part, grad_mlp_part, ff_terms = feed_forward(normed_mlp_low, all_grad_y, ff_full)
    grad_normed_mlp = scatter_tp(grad_mlp_part)
    ff_mine = lax.psum_scatter(ff_terms, FSDP, scatter_dimension=0, tiled=True)
    grad_res = grad_y + norm_back(grad_normed_mlp, residual, factor_mlp)

    grad_res_low = gather_tp(grad_res.astype(BF16))
    down_part, grad_res_low = lax.optimization_barrier((down_part, grad_res_low))
    output = residual + scatter_tp(down_part)
    grad_mixed = dot(grad_res_low, w_out_t, 1, 0)
    grad_attended = jnp.where(valid, grad_mixed, 0.0).astype(BF16).reshape(-1, q_heads, HEAD_SIZE)
    grad_attended = jnp.transpose(grad_attended, (1, 0, 2))
    grad_probs = jnp.einsum("hqd,hkd->hqk", grad_attended, values, preferred_element_type=F32)
    inner = jnp.sum(probs * grad_probs, axis=-1, keepdims=True)
    grad_scores = (probs * (grad_probs - inner)).astype(BF16)
    grad_query = jnp.einsum("hqk,hkd->qhd", grad_scores, keys, preferred_element_type=F32) * scale
    grad_keys = contract(
        jnp.einsum("hqk,hqd->hkd", grad_scores, query, preferred_element_type=F32) * scale
    )
    grad_values = contract(
        jnp.einsum("hqk,hqd->hkd", probs_low, grad_attended, preferred_element_type=F32)
    )
    grad_pairs = jnp.concatenate([grad_keys, grad_values])
    if n_ctx > 1:
        grad_pairs = lax.psum_scatter(grad_pairs, "ctx", scatter_dimension=1, tiled=True)
    grad_pairs = jnp.transpose(grad_pairs, (1, 0, 2))
    grad_turned = jnp.concatenate([grad_query, grad_pairs[:, :2]], axis=1)
    grad_lin = rotate(grad_turned, cosine, -sine, q_heads + 2)
    grad_qkv_low = (
        jnp.concatenate([grad_lin, grad_pairs[:, 2:]], axis=1).astype(BF16).reshape(-1, qkv_cols)
    )
    grad_normed_part = dot(grad_qkv_low, w_qkv, 1, 1)
    grad_normed = scatter_tp(grad_normed_part)
    grad_rows = grad_res + norm_back(grad_normed, rows, factor_attn[:own_rows])

    attn_terms = jnp.concatenate(
        [
            dot(normed_low, grad_qkv_low, 0, 0).astype(BF16),
            dot(grad_res_low, mixed, 0, 0).astype(BF16),
        ],
        axis=1,
    )
    attn_mine = lax.psum_scatter(attn_terms, FSDP, scatter_dimension=0, tiled=True)

    def owned(mine):
        blocks = [mine[t * shard_rows : (t + 1) * shard_rows] for t in range(TP)]
        return [g.astype(F32) for g in exchange_tp(blocks, me)]

    ff_grads = owned(ff_mine)
    attn_mine, *ff_grads = lax.optimization_barrier((attn_mine, *ff_grads))
    attn_grads = owned(attn_mine)

    def give_back(own_out):
        own_out = dot(own_out, order, 1, 1).astype(BF16)
        top, low = own_out[:span], own_out[span:]
        keep = jnp.where(first_core, top, low)
        got = swap_core(jnp.where(first_core, low, top))
        return jnp.stack([jnp.where(first_core, keep, got), jnp.where(first_core, got, keep)])[:, None]

    layer_out = give_back(output.astype(BF16))
    grad_tokens = give_back(grad_rows.astype(BF16))
    def kv_grad(start):
        halves = [[g[:, start + h * HEAD_SIZE : start + (h + 1) * HEAD_SIZE] for h in (0, 1)] for g in attn_grads]
        heads = [halves[0][0]]
        heads += [halves[t - 1][1] + halves[t][0] for t in range(1, TP)]
        heads += [halves[TP - 1][1]]
        return jnp.concatenate(heads, axis=1)

    def wide(grads, start, size):
        return jnp.concatenate([g[:, start : start + size] for g in grads], axis=1)

    def gain_grad(*pairs):
        return sum(jnp.sum(grad * weight.astype(F32), axis=1) for grad, weight in pairs)

    raw_query = wide(attn_grads, 0, q_cols)
    raw_key = kv_grad(q_cols)
    raw_value = kv_grad(q_cols + pair_cols)
    raw_gate = wide(ff_grads, 0, ff_cols)
    raw_up = wide(ff_grads, ff_cols, ff_cols)
    gain_attn_grad = gain_grad((raw_query, w_query), (raw_key, key_weight), (raw_value, w_value))
    gain_mlp_grad = gain_grad((raw_gate, w_gate), (raw_up, w_up))
    return (
        layer_out,
        grad_tokens,
        gain_attn_grad,
        raw_query * gain_attn_col,
        raw_key * gain_attn_col,
        raw_value * gain_attn_col,
        jnp.transpose(wide(attn_grads, qkv_cols, q_cols)),
        gain_mlp_grad,
        raw_gate * gain_mlp_col,
        raw_up * gain_mlp_col,
        jnp.transpose(wide(ff_grads, 2 * ff_cols, ff_cols)),
    )


def solution(mesh):
    n_dp, n_seq = mesh.shape["dp"], mesh.shape["seq"]
    n_ctx = n_seq // (TP * CORES)
    fine = Mesh(mesh.devices.reshape(n_dp, n_ctx, TP, CORES), ("dp", "ctx", "tp", "core"))
    seq = ("ctx", "tp", "core")
    model = ("dp", *seq)
    rows = P(None, "dp", seq, None)

    def body(*arrays):
        return local(n_dp * n_ctx, *arrays)

    return jax.shard_map(
        body,
        mesh=fine,
        in_specs=(
            rows, rows, P(None, "dp"), P(model), P(model, None), P(model, None), P(model, None),
            P(None, model), P(model), P(model, None), P(model, None), P(None, model),
        ),
        out_specs=(
            rows, rows, P(model), P(model, None), P(model, None), P(model, None), P(None, model),
            P(model), P(model, None), P(model, None), P(None, model),
        ),
        check_vma=False,
    )
```
